512 devices in a mesh: seq: 64 (over z_lo, x, core), chan: 8 (over z_hi, y).
Axes of the slice: x: 4, y: 4, z: 16 (z_hi: 2, z_lo: 8; z = z_hi * 8 + z_lo), core: 2. Of those that a mesh axis runs over, the one named last changes fastest.
Arguments:
- inputs: bfloat16 [512, 262144], P('chan', 'seq'), may hold values from -6 to 6
- gate_acts: bfloat16 [512, 262144], P('chan', 'seq'), may hold values from -6 to 6
- out_grad: bfloat16 [512, 262144], P('chan', 'seq'), may hold values from -6 to 6
- first_factor: bfloat16 [512, 512], replicated, may hold values from -0.25 to 0.25
- second_factor: bfloat16 [512, 512], replicated, may hold values from -0.25 to 0.25
Outputs:
- input_grad: bfloat16 [512, 262144], P('chan', 'seq')
- gate_grad: bfloat16 [512, 262144], P('chan', 'seq')
- first_grad: float32 [512, 512], P('seq')
- second_grad: float32 [512, 512], P('seq')
The draws below stay inside these ranges and needn't reach their ends.
All inputs are finite; a program needn't handle non-finite values.
Results may differ from the reference program's by a relative error of at most 0.0057.
Values may be sent and summed in bfloat16 or wider, within the bound.
No kernel may reach another device: no remote copies, remote signals or barrier semaphores. Data moves between devices by JAX's collectives and lax.ppermute only.
A program may use at most 64 MiB of HBM per device.

```python
import math
import jax
import jax.numpy as jnp
from jax import lax

N1 = 512
N2 = 512
CHANNELS = 512
LENGTH = 262144


def steps_of(rng, shape, cuts, least, largest):
    def one(axis_at, parts):
        draws = jax.random.uniform(jax.random.fold_in(jax.random.fold_in(rng, 6), axis_at), (parts,), jnp.float32, least / len(cuts), largest / len(cuts))
        return jnp.repeat(jnp.exp(draws), shape[axis_at] // parts).reshape((-1,) + (1,) * (len(shape) - axis_at - 1))

    level = one(*cuts[0])
    for cut in cuts[1:]:
        level = level * one(*cut)
    return level


def gaussian(rng, dims, deviation, bound, shards=(), held_as=jnp.bfloat16):
    gain = steps_of(rng, dims, shards, -0.22, 0.18) if shards else 1.0
    values = jax.random.normal(rng, dims, jnp.float32) * deviation * gain
    return jnp.minimum(jnp.maximum(values, -bound), bound).astype(held_as)


def setup_inputs(seed: int = 0) -> dict:
    keys = jax.random.split(jax.random.key(seed), 6)
    inputs = gaussian(keys[0], (CHANNELS, LENGTH), 1.0, 6.0, ((0, 8), (1, 64)))
    gate_acts = gaussian(keys[1], (CHANNELS, LENGTH), 1.0, 6.0, ((0, 8), (1, 64)))
    out_grad = gaussian(keys[2], (CHANNELS, LENGTH), 1.0, 6.0, ((0, 8), (1, 64)))
    first_factor = gaussian(keys[3], (N2, N2), N2 ** -0.5, 0.25)
    second_factor = gaussian(keys[4], (N1, N1), N1 ** -0.5, 0.25)
    return {"inputs": inputs, "gate_acts": gate_acts, "out_grad": out_grad, "first_factor": first_factor, "second_factor": second_factor}


def reference(inputs, gate_acts, out_grad, first_factor, second_factor):
    highest = lax.Precision.HIGHEST
    block_extent = math.gcd(CHANNELS, 32)
    count = CHANNELS // block_extent
    first_mat = first_factor.astype(jnp.float32)
    second_mat = second_factor.astype(jnp.float32)

    def round_keep(value):
        return lax.optimization_barrier(value.astype(jnp.bfloat16)).astype(jnp.float32)

    def step(carry, pieces):
        first_acc, second_acc = carry
        input_block, gate_block, grad_block = pieces
        grid_vals = input_block.astype(jnp.float32).reshape(block_extent, N1, N2)
        inner = round_keep(jnp.einsum('cij,kj->cik', grid_vals, first_mat, precision=highest))
        mixed_out = jnp.einsum('cik,mi->ckm', inner, second_mat, precision=highest)
        gate_vals = gate_block.astype(jnp.float32).reshape(block_extent, N2, N1)
        gradient_entries = grad_block.astype(jnp.float32).reshape(block_extent, N2, N1)
        gate_grad = (gradient_entries * mixed_out).astype(jnp.bfloat16).reshape(block_extent, N1 * N2)
        mixer_gradient = round_keep(gradient_entries * gate_vals)
        inner_grad = round_keep(jnp.einsum('ckm,mi->cik', mixer_gradient, second_mat, precision=highest))
        input_grad = jnp.einsum('cik,kj->cij', inner_grad, first_mat, precision=highest)
        input_grad = input_grad.astype(jnp.bfloat16).reshape(block_extent, N1 * N2)
        second_acc = second_acc + jnp.einsum('ckm,cik->mi', mixer_gradient, inner, precision=highest)
        first_acc = first_acc + jnp.einsum('cik,cij->kj', inner_grad, grid_vals, precision=highest)
        return (first_acc, second_acc), (input_grad, gate_grad)

    stacked = (inputs.reshape(count, block_extent, N1 * N2),
               gate_acts.reshape(count, block_extent, N1 * N2),
               out_grad.reshape(count, block_extent, N1 * N2))
    start = (jnp.zeros((N2, N2), jnp.float32), jnp.zeros((N1, N1), jnp.float32))
    (first_grad, second_grad), (input_grad, gate_grad) = lax.scan(step, start, stacked)
    return (input_grad.reshape(CHANNELS, N1 * N2), gate_grad.reshape(CHANNELS, N1 * N2),
            first_grad, second_grad)
```

```python
import jax
import jax.numpy as jnp
from jax import lax
from jax.experimental import pallas as pl
from jax.experimental.pallas import tpu as pltpu
from jax.sharding import Mesh
from jax.sharding import PartitionSpec as P

BF = jnp.bfloat16
F32 = jnp.float32
SEQ = ("zl", "x", "core")
CHAN = ("zh", "y")
LANES = 128


def dot(a, b, dims):
    return lax.dot_general(a, b, (dims, ((), ())), preferred_element_type=F32)


def stacked(ref, width):
    blocks = ref.shape[1] // width
    return jnp.concatenate([ref[:, b * width:(b + 1) * width] for b in range(blocks)], axis=0)


def product_stacked(g_ref, q_ref, width):
    blocks = g_ref.shape[1] // width
    return jnp.concatenate(
        [
            (
                g_ref[:, b * width:(b + 1) * width].astype(F32)
                * q_ref[:, b * width:(b + 1) * width].astype(F32)
            ).astype(BF)
            for b in range(blocks)
        ],
        axis=0,
    )


def send_kernel(x_ref, g_ref, q_ref, first_ref, second_ref, out_ref):
    cols = first_ref.shape[0]
    rows = second_ref.shape[0]
    count, both, width = out_ref.shape
    inner = dot(first_ref[...], stacked(x_ref, cols), ((1,), (1,)))
    mixer = product_stacked(g_ref, q_ref, rows)
    back = dot(second_ref[...], mixer, ((0,), (1,)))
    out_ref[...] = jnp.concatenate(
        [inner.reshape(count, both // 2, width), back.reshape(count, both // 2, width)], axis=1
    ).astype(BF)


def regroup(received, scratch, result):
    count, own, width = received.shape
    groups = width // LANES
    half = LANES // 2
    for group in range(groups):
        scratch[group] = received[:, :, group * LANES:(group + 1) * LANES].reshape(count * own, LANES)
    low = lax.broadcasted_iota(jnp.int32, (count, LANES), 1) < half
    for pair in range(own // 2):
        for group in range(groups):
            a = scratch[group, pl.ds(2 * pair, count, stride=own), :]
            b = scratch[group, pl.ds(2 * pair + 1, count, stride=own), :]
            result[pair, pl.ds(2 * group, count, stride=own), :] = jnp.where(low, a, pltpu.roll(b, half, 1))
            result[pair, pl.ds(2 * group + 1, count, stride=own), :] = jnp.where(low, pltpu.roll(a, half, 1), b)
    return jnp.concatenate([result[pair].astype(BF) for pair in range(own // 2)], axis=1)


def terms_kernel(recv_ref, x_ref, g_ref, q_ref, terms_ref, za_ref, zb_ref, scratch, result):
    count, both, width = recv_ref.shape
    own = both // 2
    received = recv_ref[...].astype(F32)
    za = regroup(received[:, :own], scratch, result)
    za_ref[...] = za
    zb = regroup(received[:, own:], scratch, result)
    zb_ref[...] = zb
    mixer = product_stacked(g_ref, q_ref, za.shape[0])
    first = dot(zb, stacked(x_ref, zb.shape[0]), ((1,), (0,)))
    second = dot(mixer, za, ((0,), (1,)))
    targets, lines, lanes = terms_ref.shape
    pieces = first.shape[1] // lanes
    planes = targets // pieces
    for target in range(planes):
        for piece in range(pieces):
            terms_ref[target * pieces + piece] = jnp.concatenate(
                [
                    term[(z * planes + target) * 8:(z * planes + target) * 8 + 8, piece * lanes:(piece + 1) * lanes]
                    for term in (first, second)
                    for z in range(lines // 16)
                ],
                axis=0,
            ).astype(BF)


def grads_kernel(za_ref, zb_ref, g_ref, first_ref, second_ref, input_ref, gate_ref):
    chan = g_ref.shape[0]
    rows = second_ref.shape[0]
    cols = first_ref.shape[0]
    mixed = dot(za_ref[...], second_ref[...], ((0,), (1,)))
    for k in range(mixed.shape[0] // chan):
        span = slice(k * rows, (k + 1) * rows)
        gate_ref[:, span] = (g_ref[:, span].astype(F32) * mixed[k * chan:(k + 1) * chan]).astype(BF)
    grad = dot(zb_ref[...], first_ref[...], ((0,), (0,)))
    for i in range(grad.shape[0] // chan):
        input_ref[:, i * cols:(i + 1) * cols] = grad[i * chan:(i + 1) * chan].astype(BF)


def plane_kernel(recv_ref, out_ref):
    total = recv_ref[0].astype(F32)
    for source in range(1, recv_ref.shape[0]):
        total += recv_ref[source].astype(F32)
    lines = out_ref.shape[0] // 2
    for z in range(lines):
        piece = jnp.concatenate([total[z * 8:z * 8 + 8], total[(lines + z) * 8:(lines + z) * 8 + 8]], axis=0)
        for copy in range(2):
            out_ref[2 * z + copy] = piece.astype(out_ref.dtype)


def line_kernel(recv_ref, out_ref):
    total = recv_ref[0].astype(F32)
    for source in range(1, recv_ref.shape[0]):
        total += recv_ref[source].astype(F32)
    for copy in range(out_ref.shape[0]):
        out_ref[copy] = total


def last_kernel(recv_ref, first_ref, second_ref):
    for piece in range(recv_ref.shape[0]):
        span = slice(piece * LANES, (piece + 1) * LANES)
        first_ref[:, span] = recv_ref[piece, 0:8]
        second_ref[:, span] = recv_ref[piece, 8:16]


def call(kernel, out_shape, name, scratch=(), flops=0, data=0):
    return pl.pallas_call(
        kernel,
        out_shape=out_shape,
        scratch_shapes=scratch,
        name=name,
        cost_estimate=pl.CostEstimate(flops=flops, bytes_accessed=data, transcendentals=0),
        compiler_params=pltpu.CompilerParams(vmem_limit_bytes=40 << 20),
    )


def exchange(value, axes):
    return lax.all_to_all(value, axes, split_axis=0, concat_axis=0, tiled=True)


def local(inputs, gate_acts, out_grad, first_factor, second_factor):
    count = lax.axis_size(SEQ)
    chan, extent = inputs.shape
    cols = first_factor.shape[0]
    rows = second_factor.shape[0]
    own = extent // cols
    width = own * chan
    lines, copies = lax.axis_size("zl"), lax.axis_size("zh")
    pieces = lax.axis_size("y")
    planes = count // lines
    shape = jax.ShapeDtypeStruct
    sent = call(
        send_kernel, shape((count, 2 * own, width), BF), "send", flops=2 * 2 * rows * cols * width, data=5 << 20
    )(inputs, out_grad, gate_acts, first_factor, second_factor)
    received = exchange(sent, SEQ)
    groups = width // LANES
    terms, za, zb = call(
        terms_kernel,
        (
            shape((planes * pieces, 2 * lines * 8, LANES), BF),
            shape((rows, width), BF),
            shape((cols, width), BF),
        ),
        "terms",
        scratch=[pltpu.VMEM((groups, rows, LANES), F32), pltpu.VMEM((own // 2, rows, LANES), F32)],
        flops=2 * 2 * rows * cols * width,
        data=5 << 20,
    )(received, inputs, out_grad, gate_acts)
    plane = exchange(terms, ("x", "core", "y"))
    input_grad, gate_grad = call(
        grads_kernel,
        (shape((chan, extent), BF), shape((chan, extent), BF)),
        "grads",
        flops=2 * 2 * rows * cols * width,
        data=4 << 20,
    )(za, zb, out_grad, first_factor, second_factor)
    partial = call(plane_kernel, shape((lines * copies, 16, LANES), F32), "plane_sum", data=1 << 20)(plane)
    line = exchange(partial, ("zl", "zh"))
    summed = call(line_kernel, shape((pieces, 16, LANES), F32), "line_sum", data=1 << 17)(line)
    gathered = exchange(summed, "y")
    first_grad, second_grad = call(
        last_kernel, (shape((8, cols), F32), shape((8, rows), F32)), "last", data=1 << 16
    )(gathered)
    return (input_grad, gate_grad, first_grad, second_grad)


def solution(mesh):
    fine = Mesh(mesh.devices.reshape(8, 4, 2, 2, 4), SEQ + CHAN)
    return jax.shard_map(
        local,
        mesh=fine,
        in_specs=(P(CHAN, SEQ), P(CHAN, SEQ), P(CHAN, SEQ), P(), P()),
        out_specs=(P(CHAN, SEQ), P(CHAN, SEQ), P(SEQ, None), P(SEQ, None)),
        check_vma=False,
    )
```

```python
import jax
import jax.numpy as jnp
from jax import lax
from jax.experimental import pallas as pl
from jax.experimental.pallas import tpu as pltpu
from jax.sharding import Mesh
from jax.sharding import PartitionSpec as P

BF = jnp.bfloat16
F32 = jnp.float32
SEQ = ("zl", "x", "core")
CHAN = ("zh", "y")
LANES = 128


def dot(a, b, dims):
    return lax.dot_general(a, b, (dims, ((), ())), preferred_element_type=F32)


def stacked(ref, width):
    blocks = ref.shape[1] // width
    return jnp.concatenate([ref[:, b * width:(b + 1) * width] for b in range(blocks)], axis=0)


def product_stacked(g_ref, q_ref, width):
    blocks = g_ref.shape[1] // width
    return jnp.concatenate(
        [
            (
                g_ref[:, b * width:(b + 1) * width].astype(F32)
                * q_ref[:, b * width:(b + 1) * width].astype(F32)
            ).astype(BF)
            for b in range(blocks)
        ],
        axis=0,
    )


def send_kernel(
    x_hbm, g_hbm, q_hbm, first_hbm, second_hbm, out_ref, stack_ref, mixer_ref, x_ref, g_ref, q_ref, first_ref, second_ref, sems
):
    pairs = ((x_hbm, x_ref), (first_hbm, first_ref), (g_hbm, g_ref), (q_hbm, q_ref), (second_hbm, second_ref))
    copies = [pltpu.make_async_copy(src, dst, sems.at[n]) for n, (src, dst) in enumerate(pairs)]
    for copy in copies:
        copy.start()
    cols = first_ref.shape[0]
    rows = second_ref.shape[0]
    count, both, width = out_ref.shape
    copies[0].wait()
    stack = stacked(x_ref, cols)
    stack_ref[...] = stack
    copies[1].wait()
    inner = dot(first_ref[...], stack, ((1,), (1,)))
    copies[2].wait()
    copies[3].wait()
    mixer = product_stacked(g_ref, q_ref, rows)
    mixer_ref[...] = mixer
    copies[4].wait()
    back = dot(second_ref[...], mixer, ((0,), (1,)))
    out_ref[...] = jnp.concatenate(
        [inner.reshape(count, both // 2, width), back.reshape(count, both // 2, width)], axis=1
    ).astype(BF)


def regroup(received, scratch, result):
    count, own, width = received.shape
    groups = width // LANES
    half = LANES // 2
    for group in range(groups):
        scratch[group] = received[:, :, group * LANES:(group + 1) * LANES].reshape(count * own, LANES)
    low = lax.broadcasted_iota(jnp.int32, (count, LANES), 1) < half
    for pair in range(own // 2):
        for group in range(groups):
            a = scratch[group, pl.ds(2 * pair, count, stride=own), :]
            b = scratch[group, pl.ds(2 * pair + 1, count, stride=own), :]
            result[pair, pl.ds(2 * group, count, stride=own), :] = jnp.where(low, a, pltpu.roll(b, half, 1))
            result[pair, pl.ds(2 * group + 1, count, stride=own), :] = jnp.where(low, pltpu.roll(a, half, 1), b)
    return jnp.concatenate([result[pair].astype(BF) for pair in range(own // 2)], axis=1)


def terms_kernel(recv_ref, stack_ref, mixer_ref, keep_ref, send_ref, za_ref, zb_ref, scratch, result, halves):
    count, both, width = recv_ref.shape
    own = both // 2
    received = recv_ref[...].astype(F32)
    za = regroup(received[:, :own], scratch, result)
    za_ref[...] = za
    zb = regroup(received[:, own:], scratch, result)
    zb_ref[...] = zb
    first = dot(zb, stack_ref[...], ((1,), (0,)))
    second = dot(mixer_ref[...], za, ((0,), (1,)))
    targets, lines, lanes = keep_ref.shape
    pieces = first.shape[1] // lanes
    across = targets // pieces
    for core in range(2):
        for x in range(across):
            for piece in range(pieces):
                starts = [((z * across + x) * 2 + core) * 8 for z in range(lines // 16)]
                halves[core, x * pieces + piece] = jnp.concatenate(
                    [
                        term[start:start + 8, piece * lanes:(piece + 1) * lanes]
                        for term in (first, second)
                        for start in starts
                    ],
                    axis=0,
                )
    core = lax.axis_index("core")
    keep_ref[...] = halves[core]
    send_ref[...] = halves[1 - core].astype(BF)


def pair_kernel(keep_ref, recv_ref, out_ref):
    out_ref[...] = (keep_ref[...] + recv_ref[...].astype(F32)).astype(BF)


def grads_kernel(za_ref, zb_ref, g_ref, first_ref, second_ref, input_ref, gate_ref):
    chan = g_ref.shape[0]
    rows = second_ref.shape[0]
    cols = first_ref.shape[0]
    mixed = dot(za_ref[...], second_ref[...], ((0,), (1,)))
    for k in range(mixed.shape[0] // chan):
        span = slice(k * rows, (k + 1) * rows)
        gate_ref[:, span] = (g_ref[:, span].astype(F32) * mixed[k * chan:(k + 1) * chan]).astype(BF)
    grad = dot(zb_ref[...], first_ref[...], ((0,), (0,)))
    for i in range(grad.shape[0] // chan):
        input_ref[:, i * cols:(i + 1) * cols] = grad[i * chan:(i + 1) * chan].astype(BF)


def plane_kernel(recv_ref, out_ref):
    total = recv_ref[0].astype(F32)
    for source in range(1, recv_ref.shape[0]):
        total += recv_ref[source].astype(F32)
    lines = out_ref.shape[0] // 2
    for z in range(lines):
        piece = jnp.concatenate([total[z * 8:z * 8 + 8], total[(lines + z) * 8:(lines + z) * 8 + 8]], axis=0)
        for copy in range(2):
            out_ref[2 * z + copy] = piece.astype(out_ref.dtype)


def line_kernel(recv_ref, out_ref):
    total = recv_ref[0].astype(F32)
    for source in range(1, recv_ref.shape[0]):
        total += recv_ref[source].astype(F32)
    for copy in range(out_ref.shape[0]):
        out_ref[copy] = total


def last_kernel(recv_ref, first_ref, second_ref):
    for piece in range(recv_ref.shape[0]):
        span = slice(piece * LANES, (piece + 1) * LANES)
        first_ref[:, span] = recv_ref[piece, 0:8]
        second_ref[:, span] = recv_ref[piece, 8:16]


def call(kernel, out_shape, name, scratch=(), flops=0, data=0, vmem=40 << 20, **specs):
    return pl.pallas_call(
        kernel,
        out_shape=out_shape,
        scratch_shapes=scratch,
        name=name,
        cost_estimate=pl.CostEstimate(flops=flops, bytes_accessed=data, transcendentals=0),
        compiler_params=pltpu.CompilerParams(vmem_limit_bytes=vmem),
        **specs,
    )


def exchange(value, axes):
    return lax.all_to_all(value, axes, split_axis=0, concat_axis=0, tiled=True)


def local(inputs, gate_acts, out_grad, first_factor, second_factor):
    count = lax.axis_size(SEQ)
    chan, extent = inputs.shape
    cols = first_factor.shape[0]
    rows = second_factor.shape[0]
    own = extent // cols
    width = own * chan
    lines, copies = lax.axis_size("zl"), lax.axis_size("zh")
    pieces = lax.axis_size("y")
    planes = count // lines
    shape = jax.ShapeDtypeStruct
    given = tuple(
        pltpu.with_memory_space_constraint(value, pltpu.HBM)
        for value in (inputs, out_grad, gate_acts, first_factor, second_factor)
    )
    sent, stack, mixer = call(
        send_kernel,
        (shape((count, 2 * own, width), BF), shape((width, cols), BF), shape((width, rows), BF)),
        "send",
        scratch=[pltpu.VMEM(value.shape, BF) for value in given] + [pltpu.SemaphoreType.DMA((len(given),))],
        flops=2 * 2 * rows * cols * width,
        data=5 << 20,
        in_specs=[pl.BlockSpec(memory_space=pltpu.HBM)] * len(given),
    )(*given)
    received = exchange(sent, SEQ)
    groups = width // LANES
    keep, send, za, zb = call(
        terms_kernel,
        (
            shape((planes // 2 * pieces, 2 * lines * 8, LANES), F32),
            shape((planes // 2 * pieces, 2 * lines * 8, LANES), BF),
            shape((rows, width), BF),
            shape((cols, width), BF),
        ),
        "terms",
        scratch=[
            pltpu.VMEM((groups, rows, LANES), F32),
            pltpu.VMEM((own // 2, rows, LANES), F32),
            pltpu.VMEM((2, planes // 2 * pieces, 2 * lines * 8, LANES), F32),
        ],
        flops=2 * 2 * rows * cols * width,
        data=5 << 20,
    )(received, stack, mixer)
    other = lax.ppermute(send, "core", [(0, 1), (1, 0)])
    paired = call(pair_kernel, shape(send.shape, BF), "pair_sum", data=2 << 20)(keep, other)
    plane = exchange(paired, ("x", "y"))
    input_grad, gate_grad = call(
        grads_kernel,
        (shape((chan, extent), BF), shape((chan, extent), BF)),
        "grads",
        flops=2 * 2 * rows * cols * width,
        data=4 << 20,
    )(za, zb, out_grad, first_factor, second_factor)
    partial = call(plane_kernel, shape((lines * copies, 16, LANES), BF), "plane_sum", data=1 << 20)(plane)
    line = exchange(partial, ("zl", "zh"))
    summed = call(line_kernel, shape((pieces, 16, LANES), F32), "line_sum", data=1 << 17)(line)
    gathered = exchange(summed, "y")
    first_grad, second_grad = call(
        last_kernel, (shape((8, cols), F32), shape((8, rows), F32)), "last", data=1 << 16
    )(gathered)
    return (input_grad, gate_grad, first_grad, second_grad)


def solution(mesh):
    fine = Mesh(mesh.devices.reshape(8, 4, 2, 2, 4), SEQ + CHAN)
    return jax.shard_map(
        local,
        mesh=fine,
        in_specs=(P(CHAN, SEQ), P(CHAN, SEQ), P(CHAN, SEQ), P(), P()),
        out_specs=(P(CHAN, SEQ), P(CHAN, SEQ), P(SEQ, None), P(SEQ, None)),
        check_vma=False,
    )
```

```python
import jax
import jax.numpy as jnp
from jax import lax
from jax.experimental import pallas as pl
from jax.experimental.pallas import tpu as pltpu
from jax.sharding import Mesh
from jax.sharding import PartitionSpec as P

BF = jnp.bfloat16
F32 = jnp.float32
SEQ = ("zb", "za", "x", "core")
CHAN = ("zh", "y")
LANES = 128


def dot(a, b, dims):
    return lax.dot_general(a, b, (dims, ((), ())), preferred_element_type=F32)


def stacked(ref, width):
    blocks = ref.shape[1] // width
    return jnp.concatenate([ref[:, b * width:(b + 1) * width] for b in range(blocks)], axis=0)


def product_stacked(g_ref, q_ref, width):
    blocks = g_ref.shape[1] // width
    return jnp.concatenate(
        [
            (
                g_ref[:, b * width:(b + 1) * width].astype(F32)
                * q_ref[:, b * width:(b + 1) * width].astype(F32)
            ).astype(BF)
            for b in range(blocks)
        ],
        axis=0,
    )


def send_kernel(
    x_hbm, g_hbm, q_hbm, first_hbm, second_hbm, out_ref, stack_ref, mixer_ref, g_ref, first_ref, second_ref, x_ref, q_ref, sems
):
    pairs = ((x_hbm, x_ref), (first_hbm, first_ref), (g_hbm, g_ref), (q_hbm, q_ref), (second_hbm, second_ref))
    copies = [pltpu.make_async_copy(src, dst, sems.at[n]) for n, (src, dst) in enumerate(pairs)]
    for copy in copies:
        copy.start()
    cols = first_ref.shape[0]
    rows = second_ref.shape[0]
    count, both, width = out_ref.shape
    copies[0].wait()
    stack = stacked(x_ref, cols)
    stack_ref[...] = stack
    copies[1].wait()
    inner = dot(first_ref[...], stack, ((1,), (1,)))
    copies[2].wait()
    copies[3].wait()
    mixer = product_stacked(g_ref, q_ref, rows)
    mixer_ref[...] = mixer
    copies[4].wait()
    back = dot(second_ref[...], mixer, ((0,), (1,)))
    out_ref[...] = jnp.concatenate(
        [inner.reshape(count, both // 2, width), back.reshape(count, both // 2, width)], axis=1
    ).astype(BF)


def regroup(received, scratch, result):
    count, own, width = received.shape
    groups = width // LANES
    half = LANES // 2
    for group in range(groups):
        scratch[group] = received[:, :, group * LANES:(group + 1) * LANES].reshape(count * own, LANES)
    low = lax.broadcasted_iota(jnp.int32, (count, LANES), 1) < half
    for pair in range(own // 2):
        for group in range(groups):
            a = scratch[group, pl.ds(2 * pair, count, stride=own), :]
            b = scratch[group, pl.ds(2 * pair + 1, count, stride=own), :]
            result[pair, pl.ds(2 * group, count, stride=own), :] = jnp.where(low, a, pltpu.roll(b, half, 1))
            result[pair, pl.ds(2 * group + 1, count, stride=own), :] = jnp.where(low, pltpu.roll(a, half, 1), b)
    return jnp.concatenate([result[pair].astype(BF) for pair in range(own // 2)], axis=1)


def terms_kernel(recv_ref, stack_ref, mixer_ref, keep_ref, send_ref, za_ref, zb_ref, scratch, result, terms):
    count, both, width = recv_ref.shape
    own = both // 2
    received = recv_ref[...].astype(F32)
    za = regroup(received[:, :own], scratch, result)
    za_ref[...] = za
    zb = regroup(received[:, own:], scratch, result)
    zb_ref[...] = zb
    terms[0] = dot(zb, stack_ref[...], ((1,), (0,)))
    terms[1] = dot(mixer_ref[...], za, ((0,), (1,)))
    targets, lines, lanes = keep_ref.shape
    pieces = terms.shape[2] // lanes
    blocks = lines // 16
    across = targets // (2 * pieces)
    core = lax.axis_index("core")
    for x in range(across):
        for piece in range(pieces):
            for za in range(2):
                for ref, line in ((keep_ref, core), (send_ref, 1 - core)):
                    ref[(x * pieces + piece) * 2 + za] = jnp.concatenate(
                        [
                            terms[
                                factor,
                                pl.ds(pl.multiple_of((2 * ((2 * zb + za) * across + x) + line) * 8, 8), 8),
                                piece * lanes:(piece + 1) * lanes,
                            ]
                            for factor in range(2)
                            for zb in range(blocks)
                        ],
                        axis=0,
                    ).astype(ref.dtype)


def pair_kernel(keep_ref, recv_ref, out_ref):
    out_ref[...] = (keep_ref[...] + recv_ref[...].astype(F32)).astype(BF)


def grads_kernel(za_ref, zb_ref, g_ref, first_ref, second_ref, input_ref, gate_ref):
    chan = g_ref.shape[0]
    rows = second_ref.shape[0]
    cols = first_ref.shape[0]
    mixed = dot(za_ref[...], second_ref[...], ((0,), (1,)))
    for k in range(mixed.shape[0] // chan):
        span = slice(k * rows, (k + 1) * rows)
        gate_ref[:, span] = (g_ref[:, span].astype(F32) * mixed[k * chan:(k + 1) * chan]).astype(BF)
    grad = dot(zb_ref[...], first_ref[...], ((0,), (0,)))
    for i in range(grad.shape[0] // chan):
        input_ref[:, i * cols:(i + 1) * cols] = grad[i * chan:(i + 1) * chan].astype(BF)


def block_kernel(recv_ref, out_ref):
    total = recv_ref[0].astype(F32)
    for source in range(1, recv_ref.shape[0]):
        total += recv_ref[source].astype(F32)
    blocks = recv_ref.shape[1] // 16
    copies = out_ref.shape[0] // blocks
    for zb in range(blocks):
        piece = jnp.concatenate([total[zb * 8:zb * 8 + 8], total[(blocks + zb) * 8:(blocks + zb) * 8 + 8]], axis=0)
        for copy in range(copies):
            out_ref[zb * copies + copy] = piece.astype(BF)


def last_kernel(recv_ref, first_ref, second_ref):
    pieces = first_ref.shape[1] // LANES
    for piece in range(pieces):
        total = recv_ref[piece].astype(F32)
        for source in range(1, recv_ref.shape[0] // pieces):
            total += recv_ref[source * pieces + piece].astype(F32)
        span = slice(piece * LANES, (piece + 1) * LANES)
        first_ref[:, span] = total[0:8]
        second_ref[:, span] = total[8:16]


def call(kernel, out_shape, name, scratch=(), flops=0, data=0, vmem=40 << 20, **specs):
    return pl.pallas_call(
        kernel,
        out_shape=out_shape,
        scratch_shapes=scratch,
        name=name,
        cost_estimate=pl.CostEstimate(flops=flops, bytes_accessed=data, transcendentals=0),
        compiler_params=pltpu.CompilerParams(vmem_limit_bytes=vmem),
        **specs,
    )


def exchange(value, axes):
    return lax.all_to_all(value, axes, split_axis=0, concat_axis=0, tiled=True)


def local(inputs, gate_acts, out_grad, first_factor, second_factor):
    count = lax.axis_size(SEQ)
    chan, extent = inputs.shape
    cols = first_factor.shape[0]
    rows = second_factor.shape[0]
    own = extent // cols
    width = own * chan
    blocks = lax.axis_size("zb")
    near = lax.axis_size(("x", "y", "za"))
    share = (near, 2 * blocks * 8, LANES)
    copies = lax.axis_size(("zh", "y"))
    shape = jax.ShapeDtypeStruct
    given = tuple(
        pltpu.with_memory_space_constraint(value, pltpu.HBM)
        for value in (inputs, out_grad, gate_acts, first_factor, second_factor)
    )
    sent, stack, mixer, cotangent, first_near, second_near = call(
        send_kernel,
        (
            shape((count, 2 * own, width), BF),
            shape((width, cols), BF),
            shape((width, rows), BF),
            shape(out_grad.shape, BF),
            shape(first_factor.shape, BF),
            shape(second_factor.shape, BF),
        ),
        "send",
        scratch=[pltpu.VMEM(inputs.shape, BF), pltpu.VMEM(gate_acts.shape, BF), pltpu.SemaphoreType.DMA((len(given),))],
        flops=2 * 2 * rows * cols * width,
        data=5 << 20,
        in_specs=[pl.BlockSpec(memory_space=pltpu.HBM)] * len(given),
    )(*given)
    received = exchange(sent, SEQ)
    groups = width // LANES
    keep, send, za, zb = call(
        terms_kernel,
        (
            shape(share, F32),
            shape(share, BF),
            shape((rows, width), BF),
            shape((cols, width), BF),
        ),
        "terms",
        scratch=[
            pltpu.VMEM((groups, rows, LANES), F32),
            pltpu.VMEM((own // 2, rows, LANES), F32),
            pltpu.VMEM((2, rows, cols), F32),
        ],
        flops=2 * 2 * rows * cols * width,
        data=5 << 20,
    )(received, stack, mixer)
    other = lax.ppermute(send, "core", [(0, 1), (1, 0)])
    paired = call(pair_kernel, shape(send.shape, BF), "pair_sum", data=2 << 20)(keep, other)
    input_grad, gate_grad = call(
        grads_kernel,
        (shape((chan, extent), BF), shape((chan, extent), BF)),
        "grads",
        flops=2 * 2 * rows * cols * width,
        data=4 << 20,
    )(za, zb, cotangent, first_near, second_near)
    paired, input_grad, gate_grad = lax.optimization_barrier((paired, input_grad, gate_grad))
    block = exchange(paired, ("x", "y", "za"))
    partial = call(block_kernel, shape((blocks * copies, 16, LANES), BF), "block_sum", data=1 << 20)(block)
    spread = exchange(partial, ("zb", "zh", "y"))
    first_grad, second_grad = call(
        last_kernel, (shape((8, cols), F32), shape((8, rows), F32)), "last", data=1 << 17
    )(spread)
    return (input_grad, gate_grad, first_grad, second_grad)


def solution(mesh):
    fine = Mesh(mesh.devices.reshape(4, 2, 4, 2, 2, 4), SEQ + CHAN)
    return jax.shard_map(
        local,
        mesh=fine,
        in_specs=(P(CHAN, SEQ), P(CHAN, SEQ), P(CHAN, SEQ), P(), P()),
        out_specs=(P(CHAN, SEQ), P(CHAN, SEQ), P(SEQ, None), P(SEQ, None)),
        check_vma=False,
    )
```

```python
import jax
import jax.numpy as jnp
from jax import lax
from jax.experimental import pallas as pl
from jax.experimental.pallas import tpu as pltpu
from jax.sharding import Mesh
from jax.sharding import PartitionSpec as P

BF = jnp.bfloat16
F32 = jnp.float32
SEQ = ("zb", "za", "x", "core")
CHAN = ("zh", "y")
LANES = 128


def dot(a, b, dims):
    return lax.dot_general(a, b, (dims, ((), ())), preferred_element_type=F32)


def stacked(ref, width):
    blocks = ref.shape[1] // width
    return jnp.concatenate([ref[:, b * width:(b + 1) * width] for b in range(blocks)], axis=0)


def product_stacked(g_ref, q_ref, width):
    blocks = g_ref.shape[1] // width
    return jnp.concatenate(
        [
            (
                g_ref[:, b * width:(b + 1) * width].astype(F32)
                * q_ref[:, b * width:(b + 1) * width].astype(F32)
            ).astype(BF)
            for b in range(blocks)
        ],
        axis=0,
    )


def send_kernel(
    x_hbm, g_hbm, q_hbm, first_hbm, second_hbm, out_ref, stack_ref, mixer_ref, g_ref, first_ref, second_ref, x_ref, q_ref, sems
):
    pairs = ((first_hbm, first_ref), (x_hbm, x_ref), (second_hbm, second_ref), (g_hbm, g_ref), (q_hbm, q_ref))
    copies = [pltpu.make_async_copy(src, dst, sems.at[n]) for n, (src, dst) in enumerate(pairs)]
    for copy in copies:
        copy.start()
    cols = first_ref.shape[0]
    rows = second_ref.shape[0]
    count, both, width = out_ref.shape
    copies[0].wait()
    copies[1].wait()
    stack = stacked(x_ref, cols)
    stack_ref[...] = stack
    inner = dot(first_ref[...], stack, ((1,), (1,)))
    for copy in copies[2:]:
        copy.wait()
    mixer = product_stacked(g_ref, q_ref, rows)
    mixer_ref[...] = mixer
    back = dot(second_ref[...], mixer, ((0,), (1,)))
    out_ref[...] = jnp.concatenate(
        [inner.reshape(count, both // 2, width), back.reshape(count, both // 2, width)], axis=1
    ).astype(BF)


def regroup(received, scratch, result):
    count, own, width = received.shape
    groups = width // LANES
    half = LANES // 2
    for group in range(groups):
        scratch[group] = received[:, :, group * LANES:(group + 1) * LANES].reshape(count * own, LANES)
    low = lax.broadcasted_iota(jnp.int32, (count, LANES), 1) < half
    for pair in range(own // 2):
        for group in range(groups):
            a = scratch[group, pl.ds(2 * pair, count, stride=own), :]
            b = scratch[group, pl.ds(2 * pair + 1, count, stride=own), :]
            result[pair, pl.ds(2 * group, count, stride=own), :] = jnp.where(low, a, pltpu.roll(b, half, 1))
            result[pair, pl.ds(2 * group + 1, count, stride=own), :] = jnp.where(low, pltpu.roll(a, half, 1), b)
    return jnp.concatenate([result[pair].astype(BF) for pair in range(own // 2)], axis=1)


def terms_kernel(recv_ref, stack_ref, mixer_ref, keep_ref, send_ref, za_ref, zb_ref, scratch, result, terms):
    count, both, width = recv_ref.shape
    own = both // 2
    received = recv_ref[...].astype(F32)
    za = regroup(received[:, :own], scratch, result)
    za_ref[...] = za
    zb = regroup(received[:, own:], scratch, result)
    zb_ref[...] = zb
    terms[0] = dot(zb, stack_ref[...], ((1,), (0,)))
    terms[1] = dot(mixer_ref[...], za, ((0,), (1,)))
    targets, lines, lanes = keep_ref.shape
    pieces = terms.shape[2] // lanes
    blocks = lines // 16
    across = targets // (2 * pieces)
    core = lax.axis_index("core")
    for x in range(across):
        for piece in range(pieces):
            for za in range(2):
                for ref, line in ((keep_ref, core), (send_ref, 1 - core)):
                    ref[(za * pieces + piece) * across + x] = jnp.concatenate(
                        [
                            terms[
                                factor,
                                pl.ds(pl.multiple_of((2 * ((2 * zb + za) * across + x) + line) * 8, 8), 8),
                                piece * lanes:(piece + 1) * lanes,
                            ]
                            for factor in range(2)
                            for zb in range(blocks)
                        ],
                        axis=0,
                    ).astype(ref.dtype)


def pair_kernel(keep_ref, recv_ref, out_ref):
    out_ref[...] = (keep_ref[...] + recv_ref[...].astype(F32)).astype(BF)


def grads_kernel(za_ref, zb_ref, g_ref, first_ref, second_ref, input_ref, gate_ref):
    chan = g_ref.shape[0]
    rows = second_ref.shape[0]
    cols = first_ref.shape[0]
    mixed = dot(za_ref[...], second_ref[...], ((0,), (1,)))
    for k in range(mixed.shape[0] // chan):
        span = slice(k * rows, (k + 1) * rows)
        gate_ref[:, span] = (g_ref[:, span].astype(F32) * mixed[k * chan:(k + 1) * chan]).astype(BF)
    grad = dot(zb_ref[...], first_ref[...], ((0,), (0,)))
    for i in range(grad.shape[0] // chan):
        input_ref[:, i * cols:(i + 1) * cols] = grad[i * chan:(i + 1) * chan].astype(BF)


def block_kernel(recv_ref, out_ref):
    total = recv_ref[0].astype(F32)
    for source in range(1, recv_ref.shape[0]):
        total += recv_ref[source].astype(F32)
    blocks = recv_ref.shape[1] // 16
    copies = out_ref.shape[0] // blocks
    for zb in range(blocks):
        piece = jnp.concatenate([total[zb * 8:zb * 8 + 8], total[(blocks + zb) * 8:(blocks + zb) * 8 + 8]], axis=0)
        for copy in range(copies):
            out_ref[zb * copies + copy] = piece.astype(BF)


def last_kernel(recv_ref, first_ref, second_ref):
    pieces = first_ref.shape[1] // LANES
    for piece in range(pieces):
        total = recv_ref[piece].astype(F32)
        for source in range(1, recv_ref.shape[0] // pieces):
            total += recv_ref[source * pieces + piece].astype(F32)
        span = slice(piece * LANES, (piece + 1) * LANES)
        first_ref[:, span] = total[0:8]
        second_ref[:, span] = total[8:16]


def call(kernel, out_shape, name, scratch=(), flops=0, data=0, vmem=40 << 20, **specs):
    return pl.pallas_call(
        kernel,
        out_shape=out_shape,
        scratch_shapes=scratch,
        name=name,
        cost_estimate=pl.CostEstimate(flops=flops, bytes_accessed=data, transcendentals=0),
        compiler_params=pltpu.CompilerParams(vmem_limit_bytes=vmem),
        **specs,
    )


def exchange(value, axes):
    return lax.all_to_all(value, axes, split_axis=0, concat_axis=0, tiled=True)


def local(inputs, gate_acts, out_grad, first_factor, second_factor):
    count = lax.axis_size(SEQ)
    chan, extent = inputs.shape
    cols = first_factor.shape[0]
    rows = second_factor.shape[0]
    own = extent // cols
    width = own * chan
    blocks = lax.axis_size("zb")
    near = lax.axis_size(("x", "y", "za"))
    share = (near, 2 * blocks * 8, LANES)
    copies = lax.axis_size(("zh", "y"))
    shape = jax.ShapeDtypeStruct
    given = tuple(
        pltpu.with_memory_space_constraint(value, pltpu.HBM)
        for value in (inputs, out_grad, gate_acts, first_factor, second_factor)
    )
    sent, stack, mixer, cotangent, first_near, second_near = call(
        send_kernel,
        (
            shape((count, 2 * own, width), BF),
            shape((width, cols), BF),
            shape((width, rows), BF),
            shape(out_grad.shape, BF),
            shape(first_factor.shape, BF),
            shape(second_factor.shape, BF),
        ),
        "send",
        scratch=[pltpu.VMEM(inputs.shape, BF), pltpu.VMEM(gate_acts.shape, BF), pltpu.SemaphoreType.DMA((len(given),))],
        flops=2 * 2 * rows * cols * width,
        data=5 << 20,
        in_specs=[pl.BlockSpec(memory_space=pltpu.HBM)] * len(given),
    )(*given)
    received = exchange(sent, SEQ)
    groups = width // LANES
    keep, send, za, zb = call(
        terms_kernel,
        (
            shape(share, F32),
            shape(share, BF),
            shape((rows, width), BF),
            shape((cols, width), BF),
        ),
        "terms",
        scratch=[
            pltpu.VMEM((groups, rows, LANES), F32),
            pltpu.VMEM((own // 2, rows, LANES), F32),
            pltpu.VMEM((2, rows, cols), F32),
        ],
        flops=2 * 2 * rows * cols * width,
        data=5 << 20,
    )(received, stack, mixer)
    other = lax.ppermute(send, "core", [(0, 1), (1, 0)])
    paired = call(pair_kernel, shape(send.shape, BF), "pair_sum", data=2 << 20)(keep, other)
    input_grad, gate_grad = call(
        grads_kernel,
        (shape((chan, extent), BF), shape((chan, extent), BF)),
        "grads",
        flops=2 * 2 * rows * cols * width,
        data=4 << 20,
    )(za, zb, cotangent, first_near, second_near)
    paired, input_grad, gate_grad = lax.optimization_barrier((paired, input_grad, gate_grad))
    block = exchange(paired, ("za", "y", "x"))
    partial = call(block_kernel, shape((blocks * copies, 16, LANES), BF), "block_sum", data=1 << 20)(block)
    spread = exchange(partial, ("zb", "zh", "y"))
    first_grad, second_grad = call(
        last_kernel, (shape((8, cols), F32), shape((8, rows), F32)), "last", data=1 << 17
    )(spread)
    return (input_grad, gate_grad, first_grad, second_grad)


def solution(mesh):
    fine = Mesh(mesh.devices.reshape(4, 2, 4, 2, 2, 4), SEQ + CHAN)
    return jax.shard_map(
        local,
        mesh=fine,
        in_specs=(P(CHAN, SEQ), P(CHAN, SEQ), P(CHAN, SEQ), P(), P()),
        out_specs=(P(CHAN, SEQ), P(CHAN, SEQ), P(SEQ, None), P(SEQ, None)),
        check_vma=False,
    )
```

```python
import jax
import jax.numpy as jnp
from jax import lax
from jax.experimental import pallas as pl
from jax.experimental.pallas import tpu as pltpu
from jax.sharding import Mesh
from jax.sharding import PartitionSpec as P

BF = jnp.bfloat16
F32 = jnp.float32
SEQ = ("zb", "za", "x", "core")
CHAN = ("zh", "y")
LANES = 128


def dot(a, b, dims):
    return lax.dot_general(a, b, (dims, ((), ())), preferred_element_type=F32)


def stacked(ref, width):
    blocks = ref.shape[1] // width
    return jnp.concatenate([ref[:, b * width:(b + 1) * width] for b in range(blocks)], axis=0)


def product_stacked(g_ref, q_ref, width):
    blocks = g_ref.shape[1] // width
    return jnp.concatenate(
        [
            (
                g_ref[:, b * width:(b + 1) * width].astype(F32)
                * q_ref[:, b * width:(b + 1) * width].astype(F32)
            ).astype(BF)
            for b in range(blocks)
        ],
        axis=0,
    )


def send_kernel(
    x_hbm, g_hbm, q_hbm, first_hbm, second_hbm, out_ref, stack_ref, mixer_ref, g_ref, first_ref, second_ref, x_ref, q_ref, sems
):
    pairs = ((first_hbm, first_ref), (x_hbm, x_ref), (second_hbm, second_ref), (g_hbm, g_ref), (q_hbm, q_ref))
    copies = [pltpu.make_async_copy(src, dst, sems.at[n]) for n, (src, dst) in enumerate(pairs)]
    for copy in copies:
        copy.start()
    cols = first_ref.shape[0]
    rows = second_ref.shape[0]
    count, both, width = out_ref.shape
    copies[0].wait()
    copies[1].wait()
    stack = stacked(x_ref, cols)
    stack_ref[...] = stack
    inner = dot(first_ref[...], stack, ((1,), (1,)))
    for copy in copies[2:]:
        copy.wait()
    mixer = product_stacked(g_ref, q_ref, rows)
    mixer_ref[...] = mixer
    back = dot(second_ref[...], mixer, ((0,), (1,)))
    out_ref[...] = jnp.concatenate(
        [inner.reshape(count, both // 2, width), back.reshape(count, both // 2, width)], axis=1
    ).astype(BF)


def regroup(received, scratch, result):
    count, own, width = received.shape
    groups = width // LANES
    half = LANES // 2
    for group in range(groups):
        scratch[group] = received[:, :, group * LANES:(group + 1) * LANES].reshape(count * own, LANES)
    low = lax.broadcasted_iota(jnp.int32, (count, LANES), 1) < half
    for pair in range(own // 2):
        for group in range(groups):
            a = scratch[group, pl.ds(2 * pair, count, stride=own), :]
            b = scratch[group, pl.ds(2 * pair + 1, count, stride=own), :]
            result[pair, pl.ds(2 * group, count, stride=own), :] = jnp.where(low, a, pltpu.roll(b, half, 1))
            result[pair, pl.ds(2 * group + 1, count, stride=own), :] = jnp.where(low, pltpu.roll(a, half, 1), b)
    return jnp.concatenate([result[pair].astype(BF) for pair in range(own // 2)], axis=1)


def terms_kernel(recv_ref, stack_ref, mixer_ref, keep_ref, send_ref, za_ref, zb_ref, scratch, result, terms):
    count, both, width = recv_ref.shape
    own = both // 2
    received = recv_ref[...].astype(F32)
    za = regroup(received[:, :own], scratch, result)
    za_ref[...] = za
    terms[1] = dot(mixer_ref[...], za, ((0,), (1,)))
    zb = regroup(received[:, own:], scratch, result)
    zb_ref[...] = zb
    terms[0] = dot(zb, stack_ref[...], ((1,), (0,)))
    targets, lines, lanes = keep_ref.shape
    pieces = terms.shape[2] // lanes
    blocks = lines // 16
    across = targets // (2 * pieces)
    core = lax.axis_index("core")
    for x in range(across):
        for piece in range(pieces):
            for za in range(2):
                for ref, line in ((keep_ref, core), (send_ref, 1 - core)):
                    ref[(za * pieces + piece) * across + x] = jnp.concatenate(
                        [
                            terms[
                                factor,
                                pl.ds(pl.multiple_of((2 * ((2 * zb + za) * across + x) + line) * 8, 8), 8),
                                piece * lanes:(piece + 1) * lanes,
                            ]
                            for factor in range(2)
                            for zb in range(blocks)
                        ],
                        axis=0,
                    ).astype(ref.dtype)


def pair_kernel(keep_ref, recv_ref, out_ref):
    out_ref[...] = (keep_ref[...] + recv_ref[...].astype(F32)).astype(BF)


def grads_kernel(za_ref, zb_ref, g_ref, first_ref, second_ref, input_ref, gate_ref):
    chan = g_ref.shape[0]
    rows = second_ref.shape[0]
    cols = first_ref.shape[0]
    mixed = dot(za_ref[...], second_ref[...], ((0,), (1,)))
    for k in range(mixed.shape[0] // chan):
        span = slice(k * rows, (k + 1) * rows)
        gate_ref[:, span] = (g_ref[:, span].astype(F32) * mixed[k * chan:(k + 1) * chan]).astype(BF)
    grad = dot(zb_ref[...], first_ref[...], ((0,), (0,)))
    for i in range(grad.shape[0] // chan):
        input_ref[:, i * cols:(i + 1) * cols] = grad[i * chan:(i + 1) * chan].astype(BF)


def block_kernel(recv_ref, out_ref):
    total = recv_ref[0].astype(F32)
    for source in range(1, recv_ref.shape[0]):
        total += recv_ref[source].astype(F32)
    blocks = recv_ref.shape[1] // 16
    copies = out_ref.shape[0] // blocks
    for zb in range(blocks):
        piece = jnp.concatenate([total[zb * 8:zb * 8 + 8], total[(blocks + zb) * 8:(blocks + zb) * 8 + 8]], axis=0)
        for copy in range(copies):
            out_ref[zb * copies + copy] = piece.astype(BF)


def last_kernel(recv_ref, first_ref, second_ref):
    pieces = first_ref.shape[1] // LANES
    for piece in range(pieces):
        total = recv_ref[piece].astype(F32)
        for source in range(1, recv_ref.shape[0] // pieces):
            total += recv_ref[source * pieces + piece].astype(F32)
        span = slice(piece * LANES, (piece + 1) * LANES)
        first_ref[:, span] = total[0:8]
        second_ref[:, span] = total[8:16]


def call(kernel, out_shape, name, scratch=(), flops=0, data=0, vmem=40 << 20, **specs):
    return pl.pallas_call(
        kernel,
        out_shape=out_shape,
        scratch_shapes=scratch,
        name=name,
        cost_estimate=pl.CostEstimate(flops=flops, bytes_accessed=data, transcendentals=0),
        compiler_params=pltpu.CompilerParams(vmem_limit_bytes=vmem),
        **specs,
    )


def exchange(value, axes):
    return lax.all_to_all(value, axes, split_axis=0, concat_axis=0, tiled=True)


def local(inputs, gate_acts, out_grad, first_factor, second_factor):
    count = lax.axis_size(SEQ)
    chan, extent = inputs.shape
    cols = first_factor.shape[0]
    rows = second_factor.shape[0]
    own = extent // cols
    width = own * chan
    blocks = lax.axis_size("zb")
    near = lax.axis_size(("x", "y", "za"))
    share = (near, 2 * blocks * 8, LANES)
    copies = lax.axis_size(("zh", "y"))
    shape = jax.ShapeDtypeStruct
    given = tuple(
        pltpu.with_memory_space_constraint(value, pltpu.HBM)
        for value in (inputs, out_grad, gate_acts, first_factor, second_factor)
    )
    sent, stack, mixer, cotangent, first_near, second_near = call(
        send_kernel,
        (
            shape((count, 2 * own, width), BF),
            shape((width, cols), BF),
            shape((width, rows), BF),
            shape(out_grad.shape, BF),
            shape(first_factor.shape, BF),
            shape(second_factor.shape, BF),
        ),
        "send",
        scratch=[pltpu.VMEM(inputs.shape, BF), pltpu.VMEM(gate_acts.shape, BF), pltpu.SemaphoreType.DMA((len(given),))],
        flops=2 * 2 * rows * cols * width,
        data=5 << 20,
        in_specs=[pl.BlockSpec(memory_space=pltpu.HBM)] * len(given),
    )(*given)
    received = exchange(sent, SEQ)
    groups = width // LANES
    keep, send, za, zb = call(
        terms_kernel,
        (
            shape(share, F32),
            shape(share, BF),
            shape((rows, width), BF),
            shape((cols, width), BF),
        ),
        "terms",
        scratch=[
            pltpu.VMEM((groups, rows, LANES), F32),
            pltpu.VMEM((own // 2, rows, LANES), F32),
            pltpu.VMEM((2, rows, cols), F32),
        ],
        flops=2 * 2 * rows * cols * width,
        data=5 << 20,
    )(received, stack, mixer)
    other = lax.ppermute(send, "core", [(0, 1), (1, 0)])
    paired = call(pair_kernel, shape(send.shape, BF), "pair_sum", data=2 << 20)(keep, other)
    input_grad, gate_grad = call(
        grads_kernel,
        (shape((chan, extent), BF), shape((chan, extent), BF)),
        "grads",
        flops=2 * 2 * rows * cols * width,
        data=4 << 20,
    )(za, zb, cotangent, first_near, second_near)
    paired, input_grad, gate_grad = lax.optimization_barrier((paired, input_grad, gate_grad))
    block = exchange(paired, ("za", "y", "x"))
    partial = call(block_kernel, shape((blocks * copies, 16, LANES), BF), "block_sum", data=1 << 20)(block)
    spread = exchange(partial, ("zb", "zh", "y"))
    first_grad, second_grad = call(
        last_kernel, (shape((8, cols), F32), shape((8, rows), F32)), "last", data=1 << 17
    )(spread)
    return (input_grad, gate_grad, first_grad, second_grad)


def solution(mesh):
    fine = Mesh(mesh.devices.reshape(4, 2, 4, 2, 2, 4), SEQ + CHAN)
    return jax.shard_map(
        local,
        mesh=fine,
        in_specs=(P(CHAN, SEQ), P(CHAN, SEQ), P(CHAN, SEQ), P(), P()),
        out_specs=(P(CHAN, SEQ), P(CHAN, SEQ), P(SEQ, None), P(SEQ, None)),
        check_vma=False,
    )
```
